128 devices in a mesh: ctx: 8 (over y_lo, x), head: 16 (over z, y_hi, core).
Axes of the slice: x: 4, y: 4 (y_hi: 2, y_lo: 2; y = y_hi * 2 + y_lo), z: 4, core: 2. Of those that a mesh axis runs over, the one named last changes fastest.
Arguments:
- passage_q: bfloat16 [8192, 16384], P(('ctx', 'head')), may hold values from -12 to 12
- passage_k: bfloat16 [8192, 1024], P(('ctx', 'head')), may hold values from -12 to 12
- passage_v: bfloat16 [8192, 1024], P(('ctx', 'head')), may hold values from -6 to 6
- new_q: bfloat16 [2048, 16384], P(('ctx', 'head')), may hold values from -12 to 12
- new_k: bfloat16 [2048, 1024], P(('ctx', 'head')), may hold values from -12 to 12
- new_v: bfloat16 [2048, 1024], P(('ctx', 'head')), may hold values from -6 to 6
- segments: int32 [8192], replicated, may hold values from 0 to 31, never falling along the last dimension, each value on 1 to 512 neighbouring positions
Outputs:
- passage_out: bfloat16 [8192, 16384], P(('ctx', 'head'))
- new_out: bfloat16 [2048, 16384], P(('ctx', 'head'))
The draws below stay inside these ranges and needn't reach their ends.
Inputs may be any that keep to these rules, and one draw needn't show every extreme that they name: `segments`: passages are runs of equal numbers, rising by one from run to run, each of 1 to 512 tokens; some passage has exactly 512.
All inputs are finite; a program needn't handle non-finite values.
Results may differ from the reference program's by a relative error of at most 0.008.
Values may be sent and summed in bfloat16 or wider, within the bound.
No kernel may reach another device: no remote copies, remote signals or barrier semaphores. Data moves between devices by JAX's collectives and lax.ppermute only.
A program may use at most 128 MiB of HBM per device.

```python
import math
import jax
import jax.numpy as jnp
import numpy as np
from jax import lax

QH = 128
KVH = 8
HD = 128
PT_DEV = 1024
MOST = 512
NEW = 2048
PTOK = 8192
PASSAGES = 32


def pair_draw(key, row_count, salt):
    base = jax.random.fold_in(key, salt)
    group_size = QH // KVH
    keys_main = jnp.clip(1.5 * jax.random.normal(jax.random.fold_in(base, 1), (row_count, KVH, HD), jnp.float32), -9.0, 9.0)
    query_main = jnp.clip(1.5 * jax.random.normal(jax.random.fold_in(base, 2), (row_count, KVH, group_size, HD), jnp.float32), -9.0, 9.0)
    return (query_main.reshape(row_count, QH * HD), keys_main.reshape(row_count, KVH * HD))


def draw_passage_q(key, part):
    return pair_draw(key, PTOK, 11)[0].astype(jnp.bfloat16)


def draw_passage_k(key, part):
    return pair_draw(key, PTOK, 11)[1].astype(jnp.bfloat16)


def draw_new_q(key, part):
    return pair_draw(key, NEW, 23)[0].astype(jnp.bfloat16)


def draw_new_k(key, part):
    return pair_draw(key, NEW, 23)[1].astype(jnp.bfloat16)


def block_levels(key, extent, split, smallest, top_value):
    level, own = 1.0, jax.random.fold_in(key, 6)
    for axis_at, blocks in split:
        draws = jnp.exp(jax.random.uniform(jax.random.fold_in(own, axis_at), (blocks,), jnp.float32, smallest / len(split), top_value / len(split)))
        level = level * jnp.repeat(draws, extent[axis_at] // blocks).reshape([-1 if axis == axis_at else 1 for axis in range(len(extent))])
    return level


def length_profile(count, total, bound, lean):
    weights = [(1 << 20) // math.isqrt(grade ** lean) + 1 for grade in range(2, count + 1)]
    surplus, counts = total - bound - (count - 1), [1] * (count - 1)
    while surplus > 0:
        free = [i for i in range(count - 1) if counts[i] < bound]
        pool, budget = sum([weights[i] for i in free]), surplus
        for i in free:
            addition = min(bound - counts[i], max(1, budget * weights[i] // pool), surplus)
            counts[i] = counts[i] + addition
            surplus = surplus - addition
    return np.array([bound] + counts)


def uneven_parts(own_key, count, total, most, skew):
    if count == 2:
        one = jax.random.randint(own_key, (), max(1, total - most), min(most, total - 1) + 1)
        return jnp.stack([one, total - one])
    sizes = jnp.asarray(length_profile(count, total, most, skew), jnp.int32)
    twos = (count - 1) // 2
    source_of, sink = sizes[1:1 + 2 * twos:2], sizes[2:2 + 2 * twos:2]
    room = jnp.minimum(source_of - 1, most - sink)
    moved = jax.random.randint(jax.random.fold_in(own_key, 1), (twos,), 0, 1 << 20) % (room + 1)
    sizes = sizes.at[1:1 + 2 * twos:2].set(source_of - moved).at[2:2 + 2 * twos:2].set(sink + moved)
    return sizes[jax.random.permutation(jax.random.fold_in(own_key, 2), count)]


def scatter_about(stream_key, dims, deviation, most, pieces=(), kind=jnp.bfloat16):
    entries = deviation * jax.random.normal(stream_key, dims, jnp.float32)
    if pieces:
        entries = entries * block_levels(stream_key, dims, pieces, -0.22, 0.18)
    return jnp.clip(entries, -most, most).astype(kind)


def setup_inputs(seed: int = 0) -> dict:
    splits = jax.random.split(jax.random.key(seed), 8)
    passage_q = draw_passage_q(jax.random.fold_in(splits[7], 71), 0)
    passage_k = draw_passage_k(jax.random.fold_in(splits[7], 71), 0)
    passage_v = scatter_about(splits[2], (PTOK, KVH * HD), 1.0, 6.0, ((0, 128),))
    new_q = draw_new_q(jax.random.fold_in(splits[7], 71), 0)
    new_k = draw_new_k(jax.random.fold_in(splits[7], 71), 0)
    new_v = scatter_about(splits[5], (NEW, KVH * HD), 1.0, 6.0, ((0, 128),))
    segments = jnp.searchsorted(jnp.cumsum(uneven_parts(splits[6], PASSAGES, PTOK, MOST, 2)), jnp.arange(PTOK), side="right").astype(jnp.int32)
    return {"passage_q": passage_q, "passage_k": passage_k, "passage_v": passage_v, "new_q": new_q, "new_k": new_k, "new_v": new_v, "segments": segments}


big_neg = -1.0e30


def soft_attend(scores, visible, values, form):
    masked = jnp.where(visible, scores, big_neg)
    row_max = jnp.max(masked, axis=-1, keepdims=True)
    weights = jnp.where(visible, jnp.exp(masked - row_max), 0.0)
    row_sum = jnp.sum(weights, axis=-1)
    rounded = lax.optimization_barrier(weights.astype(jnp.bfloat16)).astype(jnp.float32)
    weighted = jnp.einsum(form, rounded, values, precision=lax.Precision.HIGHEST)
    return (weighted / row_sum[..., None]).astype(jnp.bfloat16)


def reference(passage_q, passage_k, passage_v, new_q, new_k, new_v, segments):
    group_size = QH // KVH
    score_scale = HD ** -0.5
    block_rows = min(512, PT_DEV)
    pass_q = passage_q.reshape(PTOK, KVH, group_size, HD)
    pass_k = passage_k.reshape(PTOK, KVH, HD)
    pass_v = passage_v.reshape(PTOK, KVH, HD)
    keys_pad = jnp.concatenate([jnp.zeros((MOST, KVH, HD), jnp.bfloat16), pass_k], axis=0)
    vals_pad = jnp.concatenate([jnp.zeros((MOST, KVH, HD), jnp.bfloat16), pass_v], axis=0)
    seg_padded = jnp.concatenate([jnp.full((MOST,), -1, jnp.int32), segments.astype(jnp.int32)])

    def passage_block(block_id):
        first_row = (block_id * block_rows).astype(jnp.int32)
        q_block = lax.dynamic_slice_in_dim(pass_q, first_row, block_rows, 0).astype(jnp.float32)
        k_block = lax.dynamic_slice_in_dim(keys_pad, first_row, block_rows + MOST, 0).astype(jnp.float32)
        v_block = lax.dynamic_slice_in_dim(vals_pad, first_row, block_rows + MOST, 0).astype(jnp.float32)
        seg_query = lax.dynamic_slice_in_dim(seg_padded, first_row + MOST, block_rows, 0)
        seg_key = lax.dynamic_slice_in_dim(seg_padded, first_row, block_rows + MOST, 0)
        causal = jnp.arange(block_rows + MOST)[None, :] - MOST <= jnp.arange(block_rows)[:, None]
        visible = causal & (seg_query[:, None] == seg_key[None, :])
        scores = jnp.einsum('qjgd,kjd->qjgk', q_block, k_block, precision=lax.Precision.HIGHEST) * score_scale
        return soft_attend(scores, visible[:, None, None, :], v_block, 'qjgk,kjd->qjgd')

    passage_out = lax.map(passage_block, jnp.arange(PTOK // block_rows, dtype=jnp.int32))
    passage_out = passage_out.reshape(PTOK, QH * HD)

    new_block_rows = min(512, NEW)
    fresh_q = new_q.reshape(NEW, KVH, group_size, HD)
    keys_all = jnp.concatenate([pass_k, new_k.reshape(NEW, KVH, HD)], axis=0)
    vals_all = jnp.concatenate([pass_v, new_v.reshape(NEW, KVH, HD)], axis=0)
    keys_heads = jnp.transpose(keys_all, (1, 0, 2))
    vals_heads = jnp.transpose(vals_all, (1, 0, 2))

    def question_block(block_id):
        first_row = (block_id * new_block_rows).astype(jnp.int32)
        q_block = lax.dynamic_slice_in_dim(fresh_q, first_row, new_block_rows, 0)
        query_pos = first_row + jnp.arange(new_block_rows, dtype=jnp.int32)
        key_pos = jnp.arange(PTOK + NEW, dtype=jnp.int32)
        visible = (key_pos[None, :] < PTOK) | (key_pos[None, :] - PTOK <= query_pos[:, None])

        def per_head(inputs):
            q_head, k_head, v_head = inputs
            scores = jnp.einsum('qgd,kd->qgk', q_head.astype(jnp.float32), k_head.astype(jnp.float32), precision=lax.Precision.HIGHEST) * score_scale
            return soft_attend(scores, visible[:, None, :], v_head.astype(jnp.float32), 'qgk,kd->qgd')

        heads_out = lax.map(per_head, (jnp.transpose(q_block, (1, 0, 2, 3)), keys_heads, vals_heads))
        return jnp.transpose(heads_out, (1, 0, 2, 3))

    new_out = lax.map(question_block, jnp.arange(NEW // new_block_rows, dtype=jnp.int32))
    new_out = new_out.reshape(NEW, QH * HD)
    return passage_out, new_out
```

```python
import functools

import jax
import jax.numpy as jnp
from jax import lax
from jax.experimental import pallas as pl
from jax.experimental.pallas import tpu as pltpu
from jax.sharding import PartitionSpec as P

QH, KVH, HD = 128, 8, 128
GROUP = QH // KVH
PT, NT = 64, 16
BOTH = ("ctx", "head")
COUNT = 128
PEERS = 32
HEADS = 4
ROWS = PEERS * HEADS * NT
KVR = 80
BF, F32 = jnp.bfloat16, jnp.float32
NEG = -1e30
SCALE = HD**-0.5 * 1.4426950408889634
VM = pl.BlockSpec(memory_space=pltpu.VMEM)

GROUPS = [[(y * 4 + x) * 16 + h for y in range(2) for h in range(16)] for x in range(4)]
SIBLING = [(i, i ^ 1) for i in range(COUNT)]
OTHER_Y = [(i, i ^ 2) for i in range(COUNT)]
BACK1 = [(i, i + 4) for i in range(COUNT - 4)]
BACK2 = [(i, i + 8) for i in range(COUNT - 8)]


def along_x(d):
    return [(i, (i // 64) * 64 + (i // 16 + d) % 4 * 16 + i % 16) for i in range(COUNT)]


def params(**kw):
    return pltpu.CompilerParams(vmem_limit_bytes=56 * 2**20, **kw)


def pack_kv(k_ref, v_ref, nk_ref, nv_ref, out_ref, win_ref):
    for j in range(KVH):
        cols = slice(j * HD, (j + 1) * HD)
        for core in range(2):
            half = slice(32 * core, 32 * core + 32)
            new = nv_ref if core else nk_ref
            for y in range(2):
                d = y * 16 + j * 2 + core
                out_ref[d, 0:32, :] = k_ref[half, cols]
                out_ref[d, 32:64, :] = v_ref[half, cols]
                out_ref[d, 64:80, :] = new[:, cols]
    win_ref[:, : KVH * HD] = k_ref[...]
    win_ref[:, KVH * HD :] = v_ref[...]


def head_of(d, h):
    y, j, core = d // 16, d % 16 // 2, d % 2
    return j * GROUP + (y * 2 + core) * HEADS + h


def pack_q(q_ref, out_ref):
    for d in range(PEERS):
        for h in range(HEADS):
            g = head_of(d, h)
            out_ref[d, h * NT : (h + 1) * NT, :] = q_ref[:, g * HD : (g + 1) * HD]


def unpack_out(blk_ref, out_ref):
    for d in range(PEERS):
        for h in range(HEADS):
            g = head_of(d, h)
            out_ref[:, g * HD : (g + 1) * HD] = blk_ref[d, h * NT : (h + 1) * NT, :]


RB = 256


def question(chunks, s_ref, *refs):
    q_ref = refs[0]
    kv = refs[1 : 1 + 2 * chunks]
    out_ref = refs[1 + 2 * chunks]
    step = pl.program_id(0)
    core, x = s_ref[0], s_ref[1]
    q = q_ref[...]
    row = step * RB + lax.broadcasted_iota(jnp.int32, (RB, 1), 0)

    def token(src, t, at_x):
        return ((src // 16) * 4 + at_x) * 256 + (src % 16) * 16 + t

    q_tok = token(row // 64, row % 16, x)
    col = lax.broadcasted_iota(jnp.int32, (1, 512), 1)

    def update(state, k, v, visible):
        m, l, acc = state
        s = lax.dot_general(q, k, (((1,), (1,)), ((), ())), preferred_element_type=F32)
        if visible is not None:
            s = jnp.where(visible, s, NEG)
        top = jnp.max(s, axis=1, keepdims=True)
        m_new = top if m is None else jnp.maximum(m, top)
        p = jnp.exp2((s - m_new) * SCALE)
        psum = jnp.sum(p, axis=1, keepdims=True)
        pv = jnp.dot(p.astype(BF), v, preferred_element_type=F32)
        if m is None:
            return m_new, psum, pv
        a = jnp.exp2((m - m_new) * SCALE)
        return m_new, l * a + psum, acc * a + pv

    state = (None, None, None)
    for c in range(chunks):
        mine, other = kv[2 * c], kv[2 * c + 1]
        for ref in (mine, other):
            k = ref[:, 0:32, :].reshape(1024, HD)
            v = ref[:, 32:64, :].reshape(1024, HD)
            state = update(state, k, v, None)
        a = mine[:, 64:80, :].reshape(512, HD)
        b = other[:, 64:80, :].reshape(512, HD)
        first = core == 0
        k = jnp.where(first, a, b)
        v = jnp.where(first, b, a)
        k_tok = token(col // 16, col % 16, s_ref[2 + c])
        state = update(state, k, v, k_tok <= q_tok)
    m, l, acc = state
    out_ref[...] = (acc / l).astype(BF)


def passage(s_ref, q_ref, start_ref, *refs):
    wins, o_ref, bias_ref = refs[:12], refs[12], refs[13]
    @pl.when(pl.program_id(0) == 0)
    def _():
        yh, core = s_ref[0], s_ref[1]
        col = lax.broadcasted_iota(jnp.int32, (PT, 768), 1)
        blk, t = col // 64, col % 64
        side, level, flip = blk // 6, blk % 6 // 2, blk % 2
        pos = level * 256 + (yh ^ flip) * 128 + (core ^ side) * 64 + t
        q_pos = 512 + yh * 128 + core * 64 + lax.broadcasted_iota(jnp.int32, (PT, 768), 0)
        ok = (pos <= q_pos) & (pos >= start_ref[...])
        bias_ref[...] = jnp.where(ok, 0.0, NEG)

    k = jnp.concatenate([r[...] for r in wins[:6]], axis=0)
    v = jnp.concatenate([r[...] for r in wins[6:]], axis=0)
    bias = bias_ref[...]
    for part in range(4):
        q = jnp.concatenate(
            [q_ref[:, (part * 4 + h) * HD : (part * 4 + h + 1) * HD] for h in range(4)], axis=0
        )
        s = lax.dot_general(q, k, (((1,), (1,)), ((), ())), preferred_element_type=F32)
        s = (s.reshape(4, PT, 768) + bias[None]).reshape(4 * PT, 768)
        m = jnp.max(s, axis=1, keepdims=True)
        p = jnp.exp2((s - m) * SCALE)
        l = jnp.sum(p, axis=1, keepdims=True)
        o = jnp.dot(p.astype(BF), v, preferred_element_type=F32) / l
        o = o.astype(BF)
        for h in range(4):
            o_ref[:, (part * 4 + h) * HD : (part * 4 + h + 1) * HD] = o[h * PT : (h + 1) * PT]


def permute(block, route):
    return lax.ppermute(block, BOTH, route)


def exchange(blocks):
    return lax.all_to_all(
        blocks, BOTH, split_axis=0, concat_axis=0, tiled=True, axis_index_groups=GROUPS
    )


def on_device(passage_q, passage_k, passage_v, new_q, new_k, new_v, segments):
    ctx, head = lax.axis_index("ctx"), lax.axis_index("head")
    x, core, y_hi = ctx % 4, head % 2, head // 2 % 2
    shape = jax.ShapeDtypeStruct

    kv_blocks, own = pl.pallas_call(
        pack_kv,
        out_shape=(shape((PEERS, KVR, HD), BF), shape((PT, 2 * KVH * HD), BF)),
        in_specs=[VM] * 4,
        out_specs=(VM, VM),
        compiler_params=params(),
        name="pack_kv",
    )(passage_k, passage_v, new_k, new_v)
    q_blocks = pl.pallas_call(
        pack_q,
        out_shape=shape((PEERS, HEADS * NT, HD), BF),
        in_specs=[VM],
        out_specs=VM,
        compiler_params=params(),
        name="pack_q",
    )(new_q)

    kv0 = exchange(kv_blocks)
    q = exchange(q_blocks).reshape(ROWS, HD)
    chunks = [kv0] + [permute(kv0, along_x(d)) for d in (1, 3, 2)]
    pairs = []
    for c in chunks:
        pairs += [c, permute(c, SIBLING)]

    level0 = jnp.concatenate([own, permute(own, OTHER_Y)], axis=0)
    level1 = permute(level0, BACK1)
    level2 = permute(level0, BACK2)
    wins = [level2, level1, level0]
    wins += [permute(w, SIBLING) for w in wins]

    where = jnp.stack([core, x, x, (x + 3) % 4, (x + 1) % 4, (x + 2) % 4]).astype(jnp.int32)
    full = pl.BlockSpec((PEERS, KVR, HD), lambda i, s: (0, 0, 0))
    out_rows = pl.pallas_call(
        functools.partial(question, 4),
        out_shape=shape((ROWS, HD), BF),
        grid_spec=pltpu.PrefetchScalarGridSpec(
            num_scalar_prefetch=1,
            grid=(ROWS // RB,),
            in_specs=[pl.BlockSpec((RB, HD), lambda i, s: (i, 0))] + [full] * 8,
            out_specs=pl.BlockSpec((RB, HD), lambda i, s: (i, 0)),
        ),
        compiler_params=params(),
        cost_estimate=pl.CostEstimate(
            flops=4 * ROWS * 10240 * HD, bytes_accessed=8 * 2**20, transcendentals=ROWS * 10240
        ),
        name="question",
    )(where, q, *pairs)
    new_blocks = exchange(out_rows.reshape(PEERS, HEADS * NT, HD))
    new_out = pl.pallas_call(
        unpack_out,
        out_shape=shape((NT, QH * HD), BF),
        in_specs=[VM],
        out_specs=VM,
        compiler_params=params(),
        name="unpack_out",
    )(new_blocks)

    flat = ctx * 16 + head
    padded = jnp.concatenate([jnp.full((512,), -1, jnp.int32), segments])
    near = lax.dynamic_slice_in_dim(padded, flat // 4 * 256, 768, 0)
    seg_q = lax.dynamic_slice_in_dim(segments, flat * PT, PT, 0)
    start = jnp.sum((near[None, :] < seg_q[:, None]).astype(jnp.int32), axis=1, keepdims=True)
    place = jnp.stack([y_hi, core]).astype(jnp.int32)
    col = lambda i, s: (0, i)
    col_v = lambda i, s: (0, i + KVH)
    pass_out = pl.pallas_call(
        passage,
        out_shape=shape((PT, QH * HD), BF),
        grid_spec=pltpu.PrefetchScalarGridSpec(
            num_scalar_prefetch=1,
            grid=(KVH,),
            in_specs=[
                pl.BlockSpec((PT, GROUP * HD), col),
                pl.BlockSpec((PT, 1), lambda i, s: (0, 0)),
            ]
            + [pl.BlockSpec((2 * PT, HD), col)] * 6
            + [pl.BlockSpec((2 * PT, HD), col_v)] * 6,
            out_specs=pl.BlockSpec((PT, GROUP * HD), col),
            scratch_shapes=[pltpu.VMEM((PT, 768), F32)],
        ),
        compiler_params=params(),
        cost_estimate=pl.CostEstimate(
            flops=4 * PT * QH * 768 * HD, bytes_accessed=7 * 2**20, transcendentals=PT * QH * 768
        ),
        name="passage",
    )(place, passage_q, start, *wins, *wins)
    return pass_out, new_out


def solution(mesh):
    row = P(BOTH, None)
    return jax.shard_map(
        on_device,
        mesh=mesh,
        in_specs=(row,) * 6 + (P(),),
        out_specs=(row, row),
        check_vma=False,
    )
```

```python
import functools

import jax
import jax.numpy as jnp
from jax import lax
from jax.experimental import pallas as pl
from jax.experimental.pallas import tpu as pltpu
from jax.sharding import PartitionSpec as P

QH, KVH, HD = 128, 8, 128
GROUP = QH // KVH
PT, NT = 64, 16
BOTH = ("ctx", "head")
COUNT = 128
PEERS = 32
HEADS = 4
ROWS = PEERS * HEADS * NT
KVR = 80
BF, F32 = jnp.bfloat16, jnp.float32
NEG = -1e30
SCALE = HD**-0.5 * 1.4426950408889634
VM = pl.BlockSpec(memory_space=pltpu.VMEM)

GROUPS = [[(y * 4 + x) * 16 + h for y in range(2) for h in range(16)] for x in range(4)]
SIBLING = [(i, i ^ 1) for i in range(COUNT)]
OTHER_Y = [(i, i ^ 2) for i in range(COUNT)]
BACK1 = [(i, i + 4) for i in range(COUNT - 4)]
BACK2 = [(i, i + 8) for i in range(COUNT - 8)]


def along_x(d):
    return [(i, (i // 64) * 64 + (i // 16 + d) % 4 * 16 + i % 16) for i in range(COUNT)]


def params(**kw):
    return pltpu.CompilerParams(vmem_limit_bytes=56 * 2**20, **kw)


def pack(k_ref, v_ref, nk_ref, nv_ref, q_ref, out_ref):
    for j in range(KVH):
        cols = slice(j * HD, (j + 1) * HD)
        for core in range(2):
            half = slice(32 * core, 32 * core + 32)
            new = nv_ref if core else nk_ref
            for y in range(2):
                d = y * 16 + j * 2 + core
                out_ref[d, 0:32, :] = k_ref[half, cols]
                out_ref[d, 32:64, :] = v_ref[half, cols]
                out_ref[d, 64:80, :] = new[:, cols]
                for h in range(HEADS):
                    g = head_of(d, h)
                    row = KVR + h * NT
                    out_ref[d, row : row + NT, :] = q_ref[:, g * HD : (g + 1) * HD]


def head_of(d, h):
    y, j, core = d // 16, d % 16 // 2, d % 2
    return j * GROUP + (y * 2 + core) * HEADS + h


def unpack_out(blk_ref, out_ref):
    for d in range(PEERS):
        for h in range(HEADS):
            g = head_of(d, h)
            out_ref[:, g * HD : (g + 1) * HD] = blk_ref[d, h * NT : (h + 1) * NT, :]


RB, KT = 512, 512
BLOCKS = ROWS // RB
STATE = 2 * HD


def pipelined(stages, blocks, tiles, state):
    def step(t, option, fill=True, first=False):
        for r in range(blocks):
            for lag in range(stages):
                at = r - lag
                if at >= 0:
                    if fill:
                        state(lag, t, at, option)
                elif not first:
                    state(lag, t - 1, at + blocks, option)

    for n, (start, end, option) in enumerate(tiles):
        if n == 0:
            step(start, option, first=True)
            start += 1
        if end - start == 1:
            step(start, option)
        elif end > start:
            lax.fori_loop(start, end, lambda t, c, o=option: (step(t, o), c)[1], 0)
    step(tiles[-1][1], tiles[-1][2], fill=False)


def question(pieces, first, last, s_ref, *refs):
    q_ref, refs = refs[0], refs[1:]
    kv, refs = refs[: 2 * len(pieces)], refs[2 * len(pieces) :]
    if not first:
        carry, refs = refs[0], refs[1:]
    out_ref, k_s, v_s, tok_s, s_s, p_s, a_s, m_s = refs[:8]
    total = refs[8] if last else out_ref
    core, x = s_ref[0], s_ref[1]

    def token(src, t, at_x):
        return ((src // 16) * 4 + at_x) * 256 + (src % 16) * 16 + t

    old = sum(2 * peers * 32 for _, peers in pieces)
    at, fresh = 0, old
    tok_s[0] = jnp.full((8, KT), -1, jnp.int32)
    for c, (src0, peers) in enumerate(pieces):
        mine, other = kv[2 * c], kv[2 * c + 1]
        for ref in (mine, other):
            rows = slice(at, at + peers * 32)
            k_s[rows, :] = ref[:, 0:32, :].reshape(peers * 32, HD)
            v_s[rows, :HD] = ref[:, 32:64, :].reshape(peers * 32, HD)
            at += peers * 32
        keys = peers * NT
        a = mine[:, 64:80, :].reshape(keys, HD)
        b = other[:, 64:80, :].reshape(keys, HD)
        rows = slice(fresh, fresh + keys)
        k_s[rows, :] = jnp.where(core == 0, a, b)
        v_s[rows, :HD] = jnp.where(core == 0, b, a)
        col = src0 * NT + lax.broadcasted_iota(jnp.int32, (8, keys), 1)
        start = (fresh - old) % KT
        tok_s[1 + (fresh - old) // KT, :, start : start + keys] = token(
            col // 16, col % 16, s_ref[2 + c]
        )
        fresh += keys
    v_s[:, HD:] = jnp.ones((fresh, HD), BF)
    if first:
        m_s[...] = jnp.full((ROWS, HD), NEG, F32)
        total[...] = jnp.zeros((ROWS, STATE), F32)
    else:
        m_s[...] = jnp.broadcast_to(carry[:, STATE - 1 :], (ROWS, HD))
        total[...] = carry[...]
    old_tiles = old // KT
    lanes = [slice(j * HD, (j + 1) * HD) for j in range(KT // HD)]

    def keys_of(t):
        return pl.ds(t * KT if isinstance(t, int) else pl.multiple_of(t * KT, KT), KT)

    def stage(which, t, r, masked):
        slot, rows = r % 2, slice(r * RB, (r + 1) * RB)
        if which == 0:
            per = RB // (HEADS * NT)
            q = q_ref[r * per : (r + 1) * per, KVR:, :].reshape(RB, HD)
            s_s[slot] = lax.dot_general(
                q, k_s[keys_of(t), :], (((1,), (1,)), ((), ())), preferred_element_type=F32
            )
        elif which == 1:
            s = [s_s[slot, :, j] for j in lanes]
            if masked:
                row = r * RB + lax.broadcasted_iota(jnp.int32, (RB, HD), 0)
                q_tok = token(row // 64, row % 16, x)
                seen = [tok_s[t - old_tiles + 1, 0:1, j] <= q_tok for j in lanes]
                s = [jnp.where(v, a, NEG) for v, a in zip(seen, s)]
            top = jnp.max(functools.reduce(jnp.maximum, s), axis=1, keepdims=True)
            before = m_s[rows, :]
            m = jnp.maximum(before, top)
            m_s[rows, :] = m
            a_s[slot] = jnp.exp2((before - m) * SCALE)
            for j, a in zip(lanes, s):
                p_s[slot, :, j] = jnp.exp2((a - m) * SCALE).astype(BF)
        else:
            pv = jnp.dot(p_s[slot], v_s[keys_of(t), :], preferred_element_type=F32)
            a = a_s[slot]
            total[rows, :HD] = total[rows, :HD] * a + pv[:, :HD]
            total[rows, HD:] = total[rows, HD:] * a + pv[:, HD:]

    pipelined(3, BLOCKS, [(0, old_tiles, False), (old_tiles, fresh // KT, True)], stage)
    if last:
        out_ref[...] = (total[:, :HD] / total[:, HD : HD + 1]).astype(BF)
    else:
        lane = lax.broadcasted_iota(jnp.int32, (ROWS, HD), 1)
        total[:, HD:] = jnp.where(lane == HD - 1, m_s[...], total[:, HD:])


def ask(q, pieces, places, state, last):
    kinds = tuple((p[2], p[1].shape[0]) for p in pieces)
    blocks = [b for p in pieces for b in p[:2]]
    keys = sum(80 * k[1] for k in kinds)
    tiles = sum(16 * k[1] for k in kinds) // KT
    scratch = [
        pltpu.VMEM((keys, HD), BF),
        pltpu.VMEM((keys, 2 * HD), BF),
        pltpu.VMEM((1 + tiles, 8, KT), jnp.int32),
        pltpu.VMEM((2, RB, KT), F32),
        pltpu.VMEM((2, RB, KT), BF),
        pltpu.VMEM((2, RB, HD), F32),
        pltpu.VMEM((ROWS, HD), F32),
    ]
    if last:
        scratch.append(pltpu.VMEM((ROWS, STATE), F32))
    carry = [] if state is None else [state]
    return pl.pallas_call(
        functools.partial(question, kinds, state is None, last),
        out_shape=jax.ShapeDtypeStruct((ROWS, HD), BF)
        if last
        else jax.ShapeDtypeStruct((ROWS, STATE), F32),
        in_specs=[pl.BlockSpec(memory_space=pltpu.SMEM)] + [VM] * (1 + len(blocks) + len(carry)),
        out_specs=VM,
        scratch_shapes=scratch,
        compiler_params=params(),
        cost_estimate=pl.CostEstimate(
            flops=6 * ROWS * keys * HD, bytes_accessed=4 * 2**20, transcendentals=ROWS * keys
        ),
        name="question",
    )(places, q, *blocks, *carry)


PARTS, KEYS = 2, 768
PART = GROUP // PARTS


def passage(s_ref, q_ref, start_ref, *refs):
    wins, o_ref, (bias_ref, s_s, p_s) = refs[:6], refs[6], refs[7:]
    yh, core = s_ref[0], s_ref[1]
    col = lax.broadcasted_iota(jnp.int32, (PT, KEYS), 1)
    blk, t = col // 64, col % 64
    side, level, flip = blk // 6, blk % 6 // 2, blk % 2
    pos = level * 256 + (yh ^ flip) * 128 + (core ^ side) * 64 + t
    q_pos = 512 + yh * 128 + core * 64 + lax.broadcasted_iota(jnp.int32, (PT, KEYS), 0)
    bias_ref[...] = jnp.where((pos <= q_pos) & (pos >= start_ref[...]), 0.0, NEG)
    lanes = [slice(j * HD, (j + 1) * HD) for j in range(KEYS // HD)]

    def columns(j):
        return pl.ds(j * HD if isinstance(j, int) else pl.multiple_of(j * HD, HD), HD)

    def stage(which, j, part, _):
        slot = part % 2
        if which == 0:
            k = jnp.concatenate([w[:, columns(j)] for w in wins], axis=0)
            q = [q_ref[:, columns(j * GROUP + part * PART + h)] for h in range(PART)]
            s_s[slot] = lax.dot_general(
                jnp.concatenate(q, axis=0), k, (((1,), (1,)), ((), ())), preferred_element_type=F32
            )
        elif which == 1:
            for h in range(PART):
                rows = slice(h * PT, (h + 1) * PT)
                s = [s_s[slot, rows, l] + bias_ref[:, l] for l in lanes]
                m = jnp.max(functools.reduce(jnp.maximum, s), axis=1, keepdims=True)
                for l, a in zip(lanes, s):
                    p_s[slot, rows, l] = jnp.exp2((a - m) * SCALE).astype(BF)
        else:
            v = jnp.concatenate([w[:, columns(j + KVH)] for w in wins], axis=0)
            v = jnp.concatenate([v, jnp.ones_like(v)], axis=1)
            o = jnp.dot(p_s[slot], v, preferred_element_type=F32)
            o = (o[:, :HD] / o[:, HD:]).astype(BF)
            for h in range(PART):
                o_ref[:, columns(j * GROUP + part * PART + h)] = o[h * PT : (h + 1) * PT]

    pipelined(3, PARTS, [(0, KVH, None)], stage)


def passages(passage_q, start, y_hi, core, wins):
    place = jnp.stack([y_hi, core]).astype(jnp.int32)
    return pl.pallas_call(
        passage,
        out_shape=jax.ShapeDtypeStruct((PT, QH * HD), BF),
        in_specs=[pl.BlockSpec(memory_space=pltpu.SMEM)] + [VM] * 8,
        out_specs=VM,
        scratch_shapes=[
            pltpu.VMEM((PT, KEYS), F32),
            pltpu.VMEM((2, PART * PT, KEYS), F32),
            pltpu.VMEM((2, PART * PT, KEYS), BF),
        ],
        compiler_params=params(),
        cost_estimate=pl.CostEstimate(
            flops=6 * PT * QH * KEYS * HD, bytes_accessed=7 * 2**20, transcendentals=PT * QH * KEYS
        ),
        name="passage",
    )(place, passage_q, start, *wins)


def permute(block, route):
    return lax.ppermute(block, BOTH, route)


def together(*values):
    return lax.optimization_barrier(values)


def exchange(blocks):
    return lax.all_to_all(
        blocks, BOTH, split_axis=0, concat_axis=0, tiled=True, axis_index_groups=GROUPS
    )


def on_device(passage_q, passage_k, passage_v, new_q, new_k, new_v, segments):
    ctx, head = lax.axis_index("ctx"), lax.axis_index("head")
    x, core, y_hi = ctx % 4, head % 2, head // 2 % 2
    shape = jax.ShapeDtypeStruct

    blocks = pl.pallas_call(
        pack,
        out_shape=shape((PEERS, KVR + HEADS * NT, HD), BF),
        in_specs=[VM] * 5,
        out_specs=VM,
        compiler_params=params(),
        name="pack",
    )(passage_k, passage_v, new_k, new_v, new_q)
    own = jnp.concatenate([passage_k, passage_v], axis=1)
    got, other_y = together(exchange(blocks), permute(own, OTHER_Y))
    kv0 = got[:, :KVR]
    kv0_other = permute(kv0, SIBLING)
    left = permute(kv0, along_x(1))
    right = permute(kv0, along_x(3))
    level0 = jnp.concatenate([own, other_y], axis=0)
    level1 = permute(level0, BACK1)
    level2 = permute(level0, BACK2)

    places = lambda *d: jnp.stack([core, x] + [(x + i) % 4 for i in d]).astype(jnp.int32)
    state = ask(got, [(got, kv0_other, 0)], places(0), None, False)
    left, right, state = together(left, right, state)
    far = [permute(left[:16], along_x(1)), permute(right[16:], along_x(3))]
    sides = [(b, permute(b, SIBLING), 0) for b in (left, right)]
    state = ask(got, sides, places(3, 1), state, False)
    *far, level1, level2 = together(*far, level1, level2, state)[:4]
    far = [(b, permute(b, SIBLING), 16 * i) for i, b in enumerate(far)]
    wins = [level2, level1, level0]
    wins += [permute(w, SIBLING) for w in wins]
    out_rows = ask(got, far, places(2, 2), state, True)
    new_blocks = exchange(out_rows.reshape(PEERS, HEADS * NT, HD))
    new_out = pl.pallas_call(
        unpack_out,
        out_shape=shape((NT, QH * HD), BF),
        in_specs=[VM],
        out_specs=VM,
        compiler_params=params(),
        name="unpack_out",
    )(new_blocks)

    flat = ctx * 16 + head
    padded = jnp.concatenate([jnp.full((512,), -1, jnp.int32), segments])
    near = lax.dynamic_slice_in_dim(padded, flat // 4 * 256, 768, 0)
    seg_q = lax.dynamic_slice_in_dim(segments, flat * PT, PT, 0)
    start = jnp.sum((near[None, :] < seg_q[:, None]).astype(jnp.int32), axis=1, keepdims=True)
    pass_out = passages(passage_q, start, y_hi, core, wins)
    return pass_out, new_out


def solution(mesh):
    row = P(BOTH, None)
    return jax.shard_map(
        on_device,
        mesh=mesh,
        in_specs=(row,) * 6 + (P(),),
        out_specs=(row, row),
        check_vma=False,
    )
```

```python
import functools

import jax
import jax.numpy as jnp
from jax import lax
from jax.experimental import pallas as pl
from jax.experimental.pallas import tpu as pltpu
from jax.sharding import PartitionSpec as P

QH, KVH, HD = 128, 8, 128
GROUP = QH // KVH
PT, NT = 64, 16
BOTH = ("ctx", "head")
COUNT = 128
PEERS = 32
HEADS = 4
ROWS = PEERS * HEADS * NT
KVR = 80
BF, F32 = jnp.bfloat16, jnp.float32
NEG = -1e30
SCALE = HD**-0.5 * 1.4426950408889634
VM = pl.BlockSpec(memory_space=pltpu.VMEM)

GROUPS = [[(y * 4 + x) * 16 + h for y in range(2) for h in range(16)] for x in range(4)]
SIBLING = [(i, i ^ 1) for i in range(COUNT)]
OTHER_Y = [(i, i ^ 2) for i in range(COUNT)]
BACK1 = [(i, i + 4) for i in range(COUNT - 4)]
BACK2 = [(i, i + 8) for i in range(COUNT - 8)]


def along_x(d):
    return [(i, (i // 64) * 64 + (i // 16 + d) % 4 * 16 + i % 16) for i in range(COUNT)]


def params(**kw):
    return pltpu.CompilerParams(vmem_limit_bytes=56 * 2**20, **kw)


def pack_kv(k_ref, v_ref, nk_ref, nv_ref, out_ref):
    for j in range(KVH):
        cols = slice(j * HD, (j + 1) * HD)
        for core in range(2):
            half = slice(32 * core, 32 * core + 32)
            new = nv_ref if core else nk_ref
            for y in range(2):
                d = y * 16 + j * 2 + core
                out_ref[d, 0:32, :] = k_ref[half, cols]
                out_ref[d, 32:64, :] = v_ref[half, cols]
                out_ref[d, 64:80, :] = new[:, cols]


def head_of(d, h):
    y, j, core = d // 16, d % 16 // 2, d % 2
    return j * GROUP + (y * 2 + core) * HEADS + h


def pack_q(q_ref, out_ref):
    for d in range(PEERS):
        for h in range(HEADS):
            g = head_of(d, h)
            out_ref[d, h * NT : (h + 1) * NT, :] = q_ref[:, g * HD : (g + 1) * HD]


def unpack_out(blk_ref, out_ref):
    for d in range(PEERS):
        for h in range(HEADS):
            g = head_of(d, h)
            out_ref[:, g * HD : (g + 1) * HD] = blk_ref[d, h * NT : (h + 1) * NT, :]


RB, KT = 512, 512
BLOCKS = ROWS // RB
STATE = 2 * HD


def pipelined(stages, blocks, tiles, state):
    def step(t, option, fill=True, first=False):
        for r in range(blocks):
            for lag in range(stages):
                at = r - lag
                if at >= 0:
                    if fill:
                        state(lag, t, at, option)
                elif not first:
                    state(lag, t - 1, at + blocks, option)

    for n, (start, end, option) in enumerate(tiles):
        if n == 0:
            step(start, option, first=True)
            start += 1
        if end - start == 1:
            step(start, option)
        elif end > start:
            lax.fori_loop(start, end, lambda t, c, o=option: (step(t, o), c)[1], 0)
    step(tiles[-1][1], tiles[-1][2], fill=False)


def question(pieces, first, last, *refs):
    q_ref, refs = refs[0], refs[1:]
    kv, refs = refs[: 2 * len(pieces)], refs[2 * len(pieces) :]
    if not first:
        carry, refs = refs[0], refs[1:]
    out_ref, k_s, v_s, tok_s, s_s, p_s, a_s, m_s = refs[:8]
    total = refs[8] if last else out_ref
    core, x = lax.axis_index("head") % 2, lax.axis_index("ctx") % 4

    def token(src, t, at_x):
        return ((src // 16) * 4 + at_x) * 256 + (src % 16) * 16 + t

    old = sum(2 * peers * 32 for _, peers, _ in pieces)
    at, fresh = 0, old
    tok_s[0] = jnp.full((8, KT), -1, jnp.int32)
    for c, (src0, peers, away) in enumerate(pieces):
        mine, other = kv[2 * c], kv[2 * c + 1]
        for ref in (mine, other):
            rows = slice(at, at + peers * 32)
            k_s[rows, :] = ref[:, 0:32, :].reshape(peers * 32, HD)
            v_s[rows, :HD] = ref[:, 32:64, :].reshape(peers * 32, HD)
            at += peers * 32
        keys = peers * NT
        a = mine[:, 64:80, :].reshape(keys, HD)
        b = other[:, 64:80, :].reshape(keys, HD)
        rows = slice(fresh, fresh + keys)
        k_s[rows, :] = jnp.where(core == 0, a, b)
        v_s[rows, :HD] = jnp.where(core == 0, b, a)
        col = src0 * NT + lax.broadcasted_iota(jnp.int32, (8, keys), 1)
        start = (fresh - old) % KT
        tok_s[1 + (fresh - old) // KT, :, start : start + keys] = token(
            col // 16, col % 16, (x + away) % 4
        )
        fresh += keys
    v_s[:, HD:] = jnp.ones((fresh, HD), BF)
    if first:
        m_s[...] = jnp.full((ROWS, HD), NEG, F32)
        total[...] = jnp.zeros((ROWS, STATE), F32)
    else:
        m_s[...] = jnp.broadcast_to(carry[:, STATE - 1 :], (ROWS, HD))
        total[...] = carry[...]
    old_tiles = old // KT
    lanes = [slice(j * HD, (j + 1) * HD) for j in range(KT // HD)]

    def keys_of(t):
        return pl.ds(t * KT if isinstance(t, int) else pl.multiple_of(t * KT, KT), KT)

    def stage(which, t, r, masked):
        slot, rows = r % 2, slice(r * RB, (r + 1) * RB)
        if which == 0:
            per = RB // (HEADS * NT)
            q = q_ref[r * per : (r + 1) * per].reshape(RB, HD)
            s_s[slot] = lax.dot_general(
                q, k_s[keys_of(t), :], (((1,), (1,)), ((), ())), preferred_element_type=F32
            )
        elif which == 1:
            s = [s_s[slot, :, j] for j in lanes]
            if masked:
                row = r * RB + lax.broadcasted_iota(jnp.int32, (RB, HD), 0)
                q_tok = token(row // 64, row % 16, x)
                seen = [tok_s[t - old_tiles + 1, 0:1, j] <= q_tok for j in lanes]
                s = [jnp.where(v, a, NEG) for v, a in zip(seen, s)]
            top = jnp.max(functools.reduce(jnp.maximum, s), axis=1, keepdims=True)
            before = m_s[rows, :]
            m = jnp.maximum(before, top)
            m_s[rows, :] = m
            a_s[slot] = jnp.exp2((before - m) * SCALE)
            for j, a in zip(lanes, s):
                p_s[slot, :, j] = jnp.exp2((a - m) * SCALE).astype(BF)
        else:
            pv = jnp.dot(p_s[slot], v_s[keys_of(t), :], preferred_element_type=F32)
            a = a_s[slot]
            total[rows, :HD] = total[rows, :HD] * a + pv[:, :HD]
            total[rows, HD:] = total[rows, HD:] * a + pv[:, HD:]

    pipelined(3, BLOCKS, [(0, old_tiles, False), (old_tiles, fresh // KT, True)], stage)
    if last:
        out_ref[...] = (total[:, :HD] / total[:, HD : HD + 1]).astype(BF)
    else:
        lane = lax.broadcasted_iota(jnp.int32, (ROWS, HD), 1)
        total[:, HD:] = jnp.where(lane == HD - 1, m_s[...], total[:, HD:])


def ask(q, pieces, state, last):
    kinds = tuple((p[2], p[1].shape[0], p[3]) for p in pieces)
    blocks = [b for p in pieces for b in p[:2]]
    keys = sum(80 * k[1] for k in kinds)
    tiles = sum(16 * k[1] for k in kinds) // KT
    scratch = [
        pltpu.VMEM((keys, HD), BF),
        pltpu.VMEM((keys, 2 * HD), BF),
        pltpu.VMEM((1 + tiles, 8, KT), jnp.int32),
        pltpu.VMEM((2, RB, KT), F32),
        pltpu.VMEM((2, RB, KT), BF),
        pltpu.VMEM((2, RB, HD), F32),
        pltpu.VMEM((ROWS, HD), F32),
    ]
    if last:
        scratch.append(pltpu.VMEM((ROWS, STATE), F32))
    carry = [] if state is None else [state]
    return pl.pallas_call(
        functools.partial(question, kinds, state is None, last),
        out_shape=jax.ShapeDtypeStruct((ROWS, HD), BF)
        if last
        else jax.ShapeDtypeStruct((ROWS, STATE), F32),
        in_specs=[VM] * (1 + len(blocks) + len(carry)),
        out_specs=VM,
        scratch_shapes=scratch,
        compiler_params=params(),
        cost_estimate=pl.CostEstimate(
            flops=6 * ROWS * keys * HD, bytes_accessed=4 * 2**20, transcendentals=ROWS * keys
        ),
        name="question",
    )(q, *blocks, *carry)


PARTS, KEYS = 2, 640
PART = GROUP // PARTS


def passage(q_ref, start_ref, *refs):
    wins, o_ref, (bias_ref, s_s, p_s) = refs[:4], refs[4], refs[5:]
    yh, core = lax.axis_index("head") // 2 % 2, lax.axis_index("head") % 2
    col = lax.broadcasted_iota(jnp.int32, (PT, KEYS), 1)
    side, blk, t = col // 320, col // 64 % 5, col % 64
    level = jnp.where(blk < 3, 2 - blk, jnp.where(blk == 3, 1, 2 * yh))
    pos = level * 256 + (yh ^ (blk // 3)) * 128 + (core ^ side) * 64 + t
    q_pos = 512 + yh * 128 + core * 64 + lax.broadcasted_iota(jnp.int32, (PT, KEYS), 0)
    bias_ref[...] = jnp.where((pos <= q_pos) & (pos >= start_ref[...]), 0.0, NEG)
    lanes = [slice(j * HD, (j + 1) * HD) for j in range(KEYS // HD)]

    def columns(j):
        return pl.ds(j * HD if isinstance(j, int) else pl.multiple_of(j * HD, HD), HD)

    def stage(which, j, part, _):
        slot = part % 2
        if which == 0:
            k = jnp.concatenate([w[:, columns(j)] for w in wins], axis=0)
            q = [q_ref[:, columns(j * GROUP + part * PART + h)] for h in range(PART)]
            s_s[slot] = lax.dot_general(
                jnp.concatenate(q, axis=0), k, (((1,), (1,)), ((), ())), preferred_element_type=F32
            )
        elif which == 1:
            for h in range(PART):
                rows = slice(h * PT, (h + 1) * PT)
                s = [s_s[slot, rows, l] + bias_ref[:, l] for l in lanes]
                m = jnp.max(functools.reduce(jnp.maximum, s), axis=1, keepdims=True)
                for l, a in zip(lanes, s):
                    p_s[slot, rows, l] = jnp.exp2((a - m) * SCALE).astype(BF)
        else:
            v = jnp.concatenate([w[:, columns(j + KVH)] for w in wins], axis=0)
            v = jnp.concatenate([v, jnp.ones_like(v)], axis=1)
            o = jnp.dot(p_s[slot], v, preferred_element_type=F32)
            o = (o[:, :HD] / o[:, HD:]).astype(BF)
            for h in range(PART):
                o_ref[:, columns(j * GROUP + part * PART + h)] = o[h * PT : (h + 1) * PT]

    pipelined(3, PARTS, [(0, KVH, None)], stage)


def passages(passage_q, start, wins):
    return pl.pallas_call(
        passage,
        out_shape=jax.ShapeDtypeStruct((PT, QH * HD), BF),
        in_specs=[VM] * 6,
        out_specs=VM,
        scratch_shapes=[
            pltpu.VMEM((PT, KEYS), F32),
            pltpu.VMEM((2, PART * PT, KEYS), F32),
            pltpu.VMEM((2, PART * PT, KEYS), BF),
        ],
        compiler_params=params(),
        cost_estimate=pl.CostEstimate(
            flops=6 * PT * QH * KEYS * HD, bytes_accessed=7 * 2**20, transcendentals=PT * QH * KEYS
        ),
        name="passage",
    )(passage_q, start, *wins)


def permute(block, route):
    return lax.ppermute(block, BOTH, route)


def together(*values):
    return lax.optimization_barrier(values)


def exchange(blocks):
    return lax.all_to_all(
        blocks, BOTH, split_axis=0, concat_axis=0, tiled=True, axis_index_groups=GROUPS
    )


def on_device(passage_q, passage_k, passage_v, new_q, new_k, new_v, segments):
    ctx, head = lax.axis_index("ctx"), lax.axis_index("head")
    y_hi = head // 2 % 2
    shape = jax.ShapeDtypeStruct

    def packed(kernel, rows, *arrays):
        return pl.pallas_call(
            kernel,
            out_shape=shape((PEERS, rows, HD), BF),
            in_specs=[VM] * len(arrays),
            out_specs=VM,
            compiler_params=params(),
            name=kernel.__name__,
        )(*arrays)

    kv_blocks = packed(pack_kv, KVR, passage_k, passage_v, new_k, new_v)
    q_blocks = packed(pack_q, HEADS * NT, new_q)

    flat = ctx * 16 + head
    padded = jnp.concatenate([jnp.full((512,), -1, jnp.int32), segments])
    around = lax.dynamic_slice_in_dim(padded, flat // 4 * 256, 768, 0)
    seg_q = lax.dynamic_slice_in_dim(segments, flat * PT, PT, 0)
    start = jnp.sum((around[None, :] < seg_q[:, None]).astype(jnp.int32), axis=1, keepdims=True)

    own = jnp.concatenate([passage_k, passage_v], axis=1)
    kv0, q_blocks, own, start = together(exchange(kv_blocks), q_blocks, own, start)
    kv0_other = permute(kv0, SIBLING)
    left = permute(kv0, along_x(1))
    right = permute(kv0, along_x(3))
    q, left, right = together(exchange(q_blocks), left, right)
    back1, back2 = permute(own, BACK1), permute(own, BACK2)

    far = [permute(left[:16], along_x(1)), permute(right[16:], along_x(3))]
    near = [(kv0, kv0_other, 0, 0)]
    near += [(b, permute(b, SIBLING), 0, d) for b, d in ((left, 3), (right, 1))]
    state = ask(q, near, None, False)
    *far, back1, back2, state = together(*far, back1, back2, state)
    across = permute(jnp.concatenate([back1, jnp.where(y_hi == 0, own, back2)]), OTHER_Y)
    column = jnp.concatenate([own, back1, back2])
    column_other = permute(column, SIBLING)
    far = [(b, permute(b, SIBLING), 16 * i, 2) for i, b in enumerate(far)]
    out_rows = ask(q, far, state, True)
    across, column_other, out_rows = together(across, column_other, out_rows)
    wins = [column, across, column_other, permute(across, SIBLING)]
    new_blocks = exchange(out_rows.reshape(PEERS, HEADS * NT, HD))
    pass_out = passages(passage_q, start, wins)
    pass_out, new_blocks = together(pass_out, new_blocks)
    new_out = pl.pallas_call(
        unpack_out,
        out_shape=shape((NT, QH * HD), BF),
        in_specs=[VM],
        out_specs=VM,
        compiler_params=params(),
        name="unpack_out",
    )(new_blocks)

    return pass_out, new_out


def solution(mesh):
    row = P(BOTH, None)
    return jax.shard_map(
        on_device,
        mesh=mesh,
        in_specs=(row,) * 6 + (P(),),
        out_specs=(row, row),
        check_vma=False,
    )
```

```python
import functools

import jax
import jax.numpy as jnp
from jax import lax
from jax.experimental import pallas as pl
from jax.experimental.pallas import tpu as pltpu
from jax.sharding import PartitionSpec as P

QH, KVH, HD = 128, 8, 128
GROUP = QH // KVH
PT, NT = 64, 16
BOTH = ("ctx", "head")
COUNT = 128
PEERS = 32
HEADS = 4
ROWS = PEERS * HEADS * NT
KVR = 80
BF, F32 = jnp.bfloat16, jnp.float32
NEG = -1e30
SCALE = HD**-0.5 * 1.4426950408889634
VM = pl.BlockSpec(memory_space=pltpu.VMEM)

GROUPS = [[(y * 4 + x) * 16 + h for y in range(2) for h in range(16)] for x in range(4)]
SIBLING = [(i, i ^ 1) for i in range(COUNT)]
OTHER_Y = [(i, i ^ 2) for i in range(COUNT)]
BACK1 = [(i, i + 4) for i in range(COUNT - 4)]
BACK2 = [(i, i + 8) for i in range(COUNT - 8)]


def along_x(d):
    return [(i, (i // 64) * 64 + (i // 16 + d) % 4 * 16 + i % 16) for i in range(COUNT)]


def params(**kw):
    return pltpu.CompilerParams(vmem_limit_bytes=56 * 2**20, **kw)


def pack_kv(k_ref, v_ref, nk_ref, nv_ref, out_ref):
    for j in range(KVH):
        cols = slice(j * HD, (j + 1) * HD)
        for core in range(2):
            half = slice(32 * core, 32 * core + 32)
            new = nv_ref if core else nk_ref
            for y in range(2):
                d = y * 16 + j * 2 + core
                out_ref[d, 0:32, :] = k_ref[half, cols]
                out_ref[d, 32:64, :] = v_ref[half, cols]
                out_ref[d, 64:80, :] = new[:, cols]


def head_of(d, h):
    y, j, core = d // 16, d % 16 // 2, d % 2
    return j * GROUP + (y * 2 + core) * HEADS + h


def pack_q(q_ref, out_ref):
    for d in range(PEERS):
        for h in range(HEADS):
            g = head_of(d, h)
            out_ref[d, h * NT : (h + 1) * NT, :] = q_ref[:, g * HD : (g + 1) * HD]


def unpack_out(blk_ref, out_ref):
    for d in range(PEERS):
        for h in range(HEADS):
            g = head_of(d, h)
            out_ref[:, g * HD : (g + 1) * HD] = blk_ref[d, h * NT : (h + 1) * NT, :]


RB, KT = 512, 512
BLOCKS = ROWS // RB
STATE = 2 * HD


def pipelined(stages, blocks, tiles, state, unroll=1):
    def step(t, option, fill=True, first=False):
        for r in range(blocks):
            for lag in range(stages):
                at = r - lag
                if at >= 0:
                    if fill:
                        state(lag, t, at, option)
                elif not first:
                    state(lag, t - 1, at + blocks, option)

    for n, (start, end, option) in enumerate(tiles):
        if n == 0:
            step(start, option, first=True)
            start += 1
        if end - start == 1:
            step(start, option)
        elif end > start:
            lax.fori_loop(start, end, lambda t, c, o=option: (step(t, o), c)[1], 0, unroll=unroll)
    step(tiles[-1][1], tiles[-1][2], fill=False)


def question(pieces, first, last, *refs):
    q_ref, refs = refs[0], refs[1:]
    kv, refs = refs[: 2 * len(pieces)], refs[2 * len(pieces) :]
    if not first:
        carry, refs = refs[0], refs[1:]
    out_ref, k_s, v_s, tok_s, s_s, p_s, a_s, m_s = refs[:8]
    total = refs[8] if last else out_ref
    core, x = lax.axis_index("head") % 2, lax.axis_index("ctx") % 4

    def token(src, t, at_x):
        return ((src // 16) * 4 + at_x) * 256 + (src % 16) * 16 + t

    old = sum(2 * peers * 32 for _, peers, _ in pieces)
    at, fresh = 0, old
    tok_s[0] = jnp.full((8, KT), -1, jnp.int32)
    for c, (src0, peers, away) in enumerate(pieces):
        mine, other = kv[2 * c], kv[2 * c + 1]
        for ref in (mine, other):
            rows = slice(at, at + peers * 32)
            k_s[rows, :] = ref[:, 0:32, :].reshape(peers * 32, HD)
            v_s[rows, :HD] = ref[:, 32:64, :].reshape(peers * 32, HD)
            at += peers * 32
        keys = peers * NT
        a = mine[:, 64:80, :].reshape(keys, HD)
        b = other[:, 64:80, :].reshape(keys, HD)
        rows = slice(fresh, fresh + keys)
        k_s[rows, :] = jnp.where(core == 0, a, b)
        v_s[rows, :HD] = jnp.where(core == 0, b, a)
        col = src0 * NT + lax.broadcasted_iota(jnp.int32, (8, keys), 1)
        start = (fresh - old) % KT
        tok_s[1 + (fresh - old) // KT, :, start : start + keys] = token(
            col // 16, col % 16, (x + away) % 4
        )
        fresh += keys
    v_s[:, HD:] = jnp.ones((fresh, HD), BF)
    if first:
        m_s[...] = jnp.full((ROWS, HD), NEG, F32)
        total[...] = jnp.zeros((ROWS, STATE), F32)
    else:
        m_s[...] = jnp.broadcast_to(carry[:, STATE - 1 :], (ROWS, HD))
        total[...] = carry[...]
    old_tiles = old // KT
    lanes = [slice(j * HD, (j + 1) * HD) for j in range(KT // HD)]

    def keys_of(t, width):
        return pl.ds(t * KT if isinstance(t, int) else pl.multiple_of(t * KT, KT), width)

    def stage(which, t, r, masked):
        slot, rows = r % 2, slice(r * RB, (r + 1) * RB)
        early = masked and r < BLOCKS // 2
        width = KT // 2 if early else KT
        half = KT // HD // 2
        if which == 0:
            per = RB // (HEADS * NT)
            q = q_ref[r * per : (r + 1) * per].reshape(RB, HD)
            k = k_s[keys_of(t, width), :]
            s_s[slot, :, :width] = lax.dot_general(
                q, k, (((1,), (1,)), ((), ())), preferred_element_type=F32
            )
        elif which == 1:
            s = [s_s[slot, :, j] for j in lanes[: width // HD]]
            if masked:
                row = r * RB + lax.broadcasted_iota(jnp.int32, (RB, HD), 0)
                q_tok = token(row // 64, row % 16, x)
                for j in range(half) if early else range(half, 2 * half):
                    seen = tok_s[t - old_tiles + 1, 0:1, lanes[j]] <= q_tok
                    s[j] = jnp.where(seen, s[j], NEG)
            top = jnp.max(functools.reduce(jnp.maximum, s), axis=1, keepdims=True)
            before = m_s[rows, :]
            m = jnp.maximum(before, top)
            m_s[rows, :] = m
            a_s[slot] = jnp.exp2((before - m) * SCALE)
            for j, a in zip(lanes, s):
                p_s[slot, :, j] = jnp.exp2((a - m) * SCALE).astype(BF)
        else:
            v = v_s[keys_of(t, width), :]
            pv = jnp.dot(p_s[slot, :, :width], v, preferred_element_type=F32)
            a = a_s[slot]
            total[rows, :HD] = total[rows, :HD] * a + pv[:, :HD]
            total[rows, HD:] = total[rows, HD:] * a + pv[:, HD:]

    pipelined(3, BLOCKS, [(0, old_tiles, False), (old_tiles, fresh // KT, True)], stage, 2)
    if last:
        out_ref[...] = (total[:, :HD] / total[:, HD : HD + 1]).astype(BF)
    else:
        lane = lax.broadcasted_iota(jnp.int32, (ROWS, HD), 1)
        total[:, HD:] = jnp.where(lane == HD - 1, m_s[...], total[:, HD:])


def ask(q, pieces, state, last):
    kinds = tuple((p[2], p[1].shape[0], p[3]) for p in pieces)
    blocks = [b for p in pieces for b in p[:2]]
    keys = sum(80 * k[1] for k in kinds)
    tiles = sum(16 * k[1] for k in kinds) // KT
    scratch = [
        pltpu.VMEM((keys, HD), BF),
        pltpu.VMEM((keys, 2 * HD), BF),
        pltpu.VMEM((1 + tiles, 8, KT), jnp.int32),
        pltpu.VMEM((2, RB, KT), F32),
        pltpu.VMEM((2, RB, KT), BF),
        pltpu.VMEM((2, RB, HD), F32),
        pltpu.VMEM((ROWS, HD), F32),
    ]
    if last:
        scratch.append(pltpu.VMEM((ROWS, STATE), F32))
    carry = [] if state is None else [state]
    return pl.pallas_call(
        functools.partial(question, kinds, state is None, last),
        out_shape=jax.ShapeDtypeStruct((ROWS, HD), BF)
        if last
        else jax.ShapeDtypeStruct((ROWS, STATE), F32),
        in_specs=[VM] * (1 + len(blocks) + len(carry)),
        out_specs=VM,
        scratch_shapes=scratch,
        compiler_params=params(),
        cost_estimate=pl.CostEstimate(
            flops=6 * ROWS * keys * HD, bytes_accessed=4 * 2**20, transcendentals=ROWS * keys
        ),
        name="question",
    )(q, *blocks, *carry)


PARTS, KEYS = 2, 640
PART = GROUP // PARTS


def passage(q_ref, start_ref, *refs):
    wins, o_ref, (bias_ref, s_s, p_s) = refs[:4], refs[4], refs[5:]
    yh, core = lax.axis_index("head") // 2 % 2, lax.axis_index("head") % 2
    col = lax.broadcasted_iota(jnp.int32, (1, KEYS), 1)
    side, blk, t = col // 320, col // 64 % 5, col % 64
    level = jnp.where(blk < 3, 2 - blk, jnp.where(blk == 3, 1, 2 * yh))
    pos = level * 256 + (yh ^ (blk // 3)) * 128 + (core ^ side) * 64 + t
    q_pos = 512 + yh * 128 + core * 64 + lax.broadcasted_iota(jnp.int32, (PT, 1), 0)
    bias_ref[...] = jnp.where((pos <= q_pos) & (pos >= start_ref[...]), 0.0, NEG)
    lanes = [slice(j * HD, (j + 1) * HD) for j in range(KEYS // HD)]

    def columns(j):
        return pl.ds(j * HD if isinstance(j, int) else pl.multiple_of(j * HD, HD), HD)

    def stage(which, j, part, _):
        slot = part % 2
        if which == 0:
            k = jnp.concatenate([w[:, columns(j)] for w in wins], axis=0)
            q = [q_ref[:, columns(j * GROUP + part * PART + h)] for h in range(PART)]
            s_s[slot] = lax.dot_general(
                jnp.concatenate(q, axis=0), k, (((1,), (1,)), ((), ())), preferred_element_type=F32
            )
        elif which == 1:
            for h in range(PART):
                rows = slice(h * PT, (h + 1) * PT)
                s = [s_s[slot, rows, l] + bias_ref[:, l] for l in lanes]
                m = jnp.max(functools.reduce(jnp.maximum, s), axis=1, keepdims=True)
                for l, a in zip(lanes, s):
                    p_s[slot, rows, l] = jnp.exp2((a - m) * SCALE).astype(BF)
        else:
            v = jnp.concatenate([w[:, columns(j + KVH)] for w in wins], axis=0)
            v = jnp.concatenate([v, jnp.ones_like(v)], axis=1)
            o = jnp.dot(p_s[slot], v, preferred_element_type=F32)
            o = (o[:, :HD] / o[:, HD:]).astype(BF)
            for h in range(PART):
                o_ref[:, columns(j * GROUP + part * PART + h)] = o[h * PT : (h + 1) * PT]

    pipelined(3, PARTS, [(0, KVH, None)], stage)


def passages(passage_q, start, wins):
    return pl.pallas_call(
        passage,
        out_shape=jax.ShapeDtypeStruct((PT, QH * HD), BF),
        in_specs=[VM] * 6,
        out_specs=VM,
        scratch_shapes=[
            pltpu.VMEM((PT, KEYS), F32),
            pltpu.VMEM((2, PART * PT, KEYS), F32),
            pltpu.VMEM((2, PART * PT, KEYS), BF),
        ],
        compiler_params=params(),
        cost_estimate=pl.CostEstimate(
            flops=6 * PT * QH * KEYS * HD, bytes_accessed=7 * 2**20, transcendentals=PT * QH * KEYS
        ),
        name="passage",
    )(passage_q, start, *wins)


def permute(block, route):
    return lax.ppermute(block, BOTH, route)


def together(*values):
    return lax.optimization_barrier(values)


def exchange(blocks):
    return lax.all_to_all(
        blocks, BOTH, split_axis=0, concat_axis=0, tiled=True, axis_index_groups=GROUPS
    )


def on_device(passage_q, passage_k, passage_v, new_q, new_k, new_v, segments):
    ctx, head = lax.axis_index("ctx"), lax.axis_index("head")
    y_hi = head // 2 % 2
    shape = jax.ShapeDtypeStruct

    def packed(kernel, rows, *arrays):
        return pl.pallas_call(
            kernel,
            out_shape=shape((PEERS, rows, HD), BF),
            in_specs=[VM] * len(arrays),
            out_specs=VM,
            compiler_params=params(),
            name=kernel.__name__,
        )(*arrays)

    kv_blocks = packed(pack_kv, KVR, passage_k, passage_v, new_k, new_v)
    q_blocks = packed(pack_q, HEADS * NT, new_q)

    flat = ctx * 16 + head
    padded = jnp.concatenate([jnp.full((512,), -1, jnp.int32), segments])
    around = lax.dynamic_slice_in_dim(padded, flat // 4 * 256, 768, 0)
    seg_q = lax.dynamic_slice_in_dim(segments, flat * PT, PT, 0)
    start = jnp.sum((around[None, :] < seg_q[:, None]).astype(jnp.int32), axis=1, keepdims=True)

    own = jnp.concatenate([passage_k, passage_v], axis=1)
    kv0, q_blocks, own, start = together(exchange(kv_blocks), q_blocks, own, start)
    kv0_other = permute(kv0, SIBLING)
    left = permute(kv0, along_x(1))
    right = permute(kv0, along_x(3))
    q, left, right = together(exchange(q_blocks), left, right)
    back1, back2 = permute(own, BACK1), permute(own, BACK2)

    far = [permute(left[:16], along_x(1)), permute(right[16:], along_x(3))]
    near = [(kv0, kv0_other, 0, 0)]
    near += [(b, permute(b, SIBLING), 0, d) for b, d in ((left, 3), (right, 1))]
    state = ask(q, near, None, False)
    *far, back1, back2, state = together(*far, back1, back2, state)
    across = permute(jnp.concatenate([back1, jnp.where(y_hi == 0, own, back2)]), OTHER_Y)
    column = jnp.concatenate([own, back1, back2])
    column_other = permute(column, SIBLING)
    far = [(b, permute(b, SIBLING), 16 * i, 2) for i, b in enumerate(far)]
    out_rows = ask(q, far, state, True)
    across, column_other, out_rows = together(across, column_other, out_rows)
    wins = [column, across, column_other, permute(across, SIBLING)]
    new_blocks = exchange(out_rows.reshape(PEERS, HEADS * NT, HD))
    pass_out = passages(passage_q, start, wins)
    pass_out, new_blocks = together(pass_out, new_blocks)
    new_out = pl.pallas_call(
        unpack_out,
        out_shape=shape((NT, QH * HD), BF),
        in_specs=[VM],
        out_specs=VM,
        compiler_params=params(),
        name="unpack_out",
    )(new_blocks)

    return pass_out, new_out


def solution(mesh):
    row = P(BOTH, None)
    return jax.shard_map(
        on_device,
        mesh=mesh,
        in_specs=(row,) * 6 + (P(),),
        out_specs=(row, row),
        check_vma=False,
    )
```

```python
import functools

import jax
import jax.numpy as jnp
from jax import lax
from jax.experimental import pallas as pl
from jax.experimental.pallas import tpu as pltpu
from jax.sharding import PartitionSpec as P

QH, KVH, HD = 128, 8, 128
GROUP = QH // KVH
PT, NT = 64, 16
BOTH = ("ctx", "head")
COUNT = 128
PEERS = 32
HEADS = 4
ROWS = PEERS * HEADS * NT
KVR = 80
BF, F32 = jnp.bfloat16, jnp.float32
NEG = -1e30
SCALE = HD**-0.5 * 1.4426950408889634
VM = pl.BlockSpec(memory_space=pltpu.VMEM)

GROUPS = [[(y * 4 + x) * 16 + h for y in range(2) for h in range(16)] for x in range(4)]
SIBLING = [(i, i ^ 1) for i in range(COUNT)]
OTHER_Y = [(i, i ^ 2) for i in range(COUNT)]
BACK1 = [(i, i + 4) for i in range(COUNT - 4)]
BACK2 = [(i, i + 8) for i in range(COUNT - 8)]


def along_x(d):
    return [(i, (i // 64) * 64 + (i // 16 + d) % 4 * 16 + i % 16) for i in range(COUNT)]


def params(**kw):
    return pltpu.CompilerParams(vmem_limit_bytes=56 * 2**20, **kw)


def pack_kv(k_ref, v_ref, nk_ref, nv_ref, out_ref):
    for j in range(KVH):
        cols = slice(j * HD, (j + 1) * HD)
        for core in range(2):
            half = slice(32 * core, 32 * core + 32)
            new = nv_ref if core else nk_ref
            for y in range(2):
                d = y * 16 + j * 2 + core
                out_ref[d, 0:32, :] = k_ref[half, cols]
                out_ref[d, 32:64, :] = v_ref[half, cols]
                out_ref[d, 64:80, :] = new[:, cols]


def head_of(d, h):
    y, j, core = d // 16, d % 16 // 2, d % 2
    return j * GROUP + (y * 2 + core) * HEADS + h


def pack_q(q_ref, out_ref):
    for d in range(PEERS):
        for h in range(HEADS):
            g = head_of(d, h)
            out_ref[d, h * NT : (h + 1) * NT, :] = q_ref[:, g * HD : (g + 1) * HD]


RB, KT = 512, 512
BLOCKS = ROWS // RB
STATE = 2 * HD


def pipelined(stages, blocks, tiles, state, unroll=1):
    def step(t, option, fill=True, first=False):
        for r in range(blocks):
            for lag in range(stages):
                at = r - lag
                if at >= 0:
                    if fill:
                        state(lag, t, at, option)
                elif not first:
                    state(lag, t - 1, at + blocks, option)

    for n, (start, end, option) in enumerate(tiles):
        if n == 0:
            step(start, option, first=True)
            start += 1
        if end - start == 1:
            step(start, option)
        elif end > start:
            lax.fori_loop(start, end, lambda t, c, o=option: (step(t, o), c)[1], 0, unroll=unroll)
    step(tiles[-1][1], tiles[-1][2], fill=False)


def question(pieces, first, last, *refs):
    q_ref, refs = refs[0], refs[1:]
    kv, refs = refs[: 2 * len(pieces)], refs[2 * len(pieces) :]
    if not first:
        carry, refs = refs[0], refs[1:]
    out_ref, k_s, v_s, tok_s, s_s, p_s, a_s, m_s = refs[:8]
    total = refs[8] if last else out_ref
    core, x = lax.axis_index("head") % 2, lax.axis_index("ctx") % 4

    def token(src, t, at_x):
        return ((src // 16) * 4 + at_x) * 256 + (src % 16) * 16 + t

    old = sum(2 * peers * 32 for _, peers, _ in pieces)
    at, fresh = 0, old
    tok_s[0] = jnp.full((8, KT), -1, jnp.int32)
    for c, (src0, peers, away) in enumerate(pieces):
        mine, other = kv[2 * c], kv[2 * c + 1]
        for ref in (mine, other):
            rows = slice(at, at + peers * 32)
            k_s[rows, :] = ref[:, 0:32, :].reshape(peers * 32, HD)
            v_s[rows, :HD] = ref[:, 32:64, :].reshape(peers * 32, HD)
            at += peers * 32
        keys = peers * NT
        a = mine[:, 64:80, :].reshape(keys, HD)
        b = other[:, 64:80, :].reshape(keys, HD)
        rows = slice(fresh, fresh + keys)
        k_s[rows, :] = jnp.where(core == 0, a, b)
        v_s[rows, :HD] = jnp.where(core == 0, b, a)
        col = src0 * NT + lax.broadcasted_iota(jnp.int32, (8, keys), 1)
        start = (fresh - old) % KT
        tok_s[1 + (fresh - old) // KT, :, start : start + keys] = token(
            col // 16, col % 16, (x + away) % 4
        )
        fresh += keys
    v_s[:, HD:] = jnp.ones((fresh, HD), BF)
    if first:
        m_s[...] = jnp.full((ROWS, HD), NEG, F32)
        total[...] = jnp.zeros((ROWS, STATE), F32)
    else:
        m_s[...] = jnp.broadcast_to(carry[:, STATE - 1 :], (ROWS, HD))
        total[...] = carry[...]
    old_tiles = old // KT
    lanes = [slice(j * HD, (j + 1) * HD) for j in range(KT // HD)]

    def keys_of(t, width):
        return pl.ds(t * KT if isinstance(t, int) else pl.multiple_of(t * KT, KT), width)

    def stage(which, t, r, masked):
        slot, rows = r % 2, slice(r * RB, (r + 1) * RB)
        early = masked and r < BLOCKS // 2
        width = KT // 2 if early else KT
        half = KT // HD // 2
        if which == 0:
            per = RB // (HEADS * NT)
            q = q_ref[r * per : (r + 1) * per].reshape(RB, HD)
            k = k_s[keys_of(t, width), :]
            s_s[slot, :, :width] = lax.dot_general(
                q, k, (((1,), (1,)), ((), ())), preferred_element_type=F32
            )
        elif which == 1:
            s = [s_s[slot, :, j] for j in lanes[: width // HD]]
            if masked:
                row = r * RB + lax.broadcasted_iota(jnp.int32, (RB, HD), 0)
                q_tok = token(row // 64, row % 16, x)
                for j in range(half) if early else range(half, 2 * half):
                    seen = tok_s[t - old_tiles + 1, 0:1, lanes[j]] <= q_tok
                    s[j] = jnp.where(seen, s[j], NEG)
            top = jnp.max(functools.reduce(jnp.maximum, s), axis=1, keepdims=True)
            before = m_s[rows, :]
            m = jnp.maximum(before, top)
            m_s[rows, :] = m
            a_s[slot] = jnp.exp2((before - m) * SCALE)
            for j, a in zip(lanes, s):
                p_s[slot, :, j] = jnp.exp2((a - m) * SCALE).astype(BF)
        else:
            v = v_s[keys_of(t, width), :]
            pv = jnp.dot(p_s[slot, :, :width], v, preferred_element_type=F32)
            a = a_s[slot]
            total[rows, :HD] = total[rows, :HD] * a + pv[:, :HD]
            total[rows, HD:] = total[rows, HD:] * a + pv[:, HD:]

    pipelined(3, BLOCKS, [(0, old_tiles, False), (old_tiles, fresh // KT, True)], stage, 2)
    if last:
        out_ref[...] = (total[:, :HD] / total[:, HD : HD + 1]).astype(BF)
    else:
        lane = lax.broadcasted_iota(jnp.int32, (ROWS, HD), 1)
        total[:, HD:] = jnp.where(lane == HD - 1, m_s[...], total[:, HD:])


def ask(q, pieces, state, last):
    kinds = tuple((p[2], p[1].shape[0], p[3]) for p in pieces)
    blocks = [b for p in pieces for b in p[:2]]
    keys = sum(80 * k[1] for k in kinds)
    tiles = sum(16 * k[1] for k in kinds) // KT
    scratch = [
        pltpu.VMEM((keys, HD), BF),
        pltpu.VMEM((keys, 2 * HD), BF),
        pltpu.VMEM((1 + tiles, 8, KT), jnp.int32),
        pltpu.VMEM((2, RB, KT), F32),
        pltpu.VMEM((2, RB, KT), BF),
        pltpu.VMEM((2, RB, HD), F32),
        pltpu.VMEM((ROWS, HD), F32),
    ]
    if last:
        scratch.append(pltpu.VMEM((ROWS, STATE), F32))
    carry = [] if state is None else [state]
    return pl.pallas_call(
        functools.partial(question, kinds, state is None, last),
        out_shape=jax.ShapeDtypeStruct((ROWS, HD), BF)
        if last
        else jax.ShapeDtypeStruct((ROWS, STATE), F32),
        in_specs=[VM] * (1 + len(blocks) + len(carry)),
        out_specs=VM,
        scratch_shapes=scratch,
        compiler_params=params(),
        cost_estimate=pl.CostEstimate(
            flops=6 * ROWS * keys * HD, bytes_accessed=4 * 2**20, transcendentals=ROWS * keys
        ),
        name="question",
    )(q, *blocks, *carry)


PARTS, KEYS = 2, 640
PART = GROUP // PARTS


def passage(q_ref, start_ref, *refs):
    wins, o_ref, (bias_ref, s_s, p_s) = refs[:4], refs[4], refs[5:]
    yh, core = lax.axis_index("head") // 2 % 2, lax.axis_index("head") % 2
    col = lax.broadcasted_iota(jnp.int32, (1, KEYS), 1)
    side, blk, t = col // 320, col // 64 % 5, col % 64
    level = jnp.where(blk < 3, 2 - blk, jnp.where(blk == 3, 1, 2 * yh))
    pos = level * 256 + (yh ^ (blk // 3)) * 128 + (core ^ side) * 64 + t
    q_pos = 512 + yh * 128 + core * 64 + lax.broadcasted_iota(jnp.int32, (PT, 1), 0)
    bias_ref[...] = jnp.where((pos <= q_pos) & (pos >= start_ref[...]), 0.0, NEG)
    lanes = [slice(j * HD, (j + 1) * HD) for j in range(KEYS // HD)]

    def columns(j):
        return pl.ds(j * HD if isinstance(j, int) else pl.multiple_of(j * HD, HD), HD)

    def stage(which, j, part, _):
        slot = part % 2
        if which == 0:
            k = jnp.concatenate([w[:, columns(j)] for w in wins], axis=0)
            q = [q_ref[:, columns(j * GROUP + part * PART + h)] for h in range(PART)]
            s_s[slot] = lax.dot_general(
                jnp.concatenate(q, axis=0), k, (((1,), (1,)), ((), ())), preferred_element_type=F32
            )
        elif which == 1:
            for h in range(PART):
                rows = slice(h * PT, (h + 1) * PT)
                s = [s_s[slot, rows, l] + bias_ref[:, l] for l in lanes]
                m = jnp.max(functools.reduce(jnp.maximum, s), axis=1, keepdims=True)
                for l, a in zip(lanes, s):
                    p_s[slot, rows, l] = jnp.exp2((a - m) * SCALE).astype(BF)
        else:
            v = jnp.concatenate([w[:, columns(j + KVH)] for w in wins], axis=0)
            v = jnp.concatenate([v, jnp.ones_like(v)], axis=1)
            o = jnp.dot(p_s[slot], v, preferred_element_type=F32)
            o = (o[:, :HD] / o[:, HD:]).astype(BF)
            for h in range(PART):
                o_ref[:, columns(j * GROUP + part * PART + h)] = o[h * PT : (h + 1) * PT]

    pipelined(3, PARTS, [(0, KVH, None)], stage)


def passages(passage_q, start, wins):
    return pl.pallas_call(
        passage,
        out_shape=jax.ShapeDtypeStruct((PT, QH * HD), BF),
        in_specs=[VM] * 6,
        out_specs=VM,
        scratch_shapes=[
            pltpu.VMEM((PT, KEYS), F32),
            pltpu.VMEM((2, PART * PT, KEYS), F32),
            pltpu.VMEM((2, PART * PT, KEYS), BF),
        ],
        compiler_params=params(),
        cost_estimate=pl.CostEstimate(
            flops=6 * PT * QH * KEYS * HD, bytes_accessed=7 * 2**20, transcendentals=PT * QH * KEYS
        ),
        name="passage",
    )(passage_q, start, *wins)


def permute(block, route):
    return lax.ppermute(block, BOTH, route)


def together(*values):
    return lax.optimization_barrier(values)


def exchange(blocks):
    return lax.all_to_all(
        blocks, BOTH, split_axis=0, concat_axis=0, tiled=True, axis_index_groups=GROUPS
    )


def on_device(passage_q, passage_k, passage_v, new_q, new_k, new_v, segments):
    ctx, head = lax.axis_index("ctx"), lax.axis_index("head")
    y_hi = head // 2 % 2
    shape = jax.ShapeDtypeStruct

    def packed(kernel, rows, *arrays):
        return pl.pallas_call(
            kernel,
            out_shape=shape((PEERS, rows, HD), BF),
            in_specs=[VM] * len(arrays),
            out_specs=VM,
            compiler_params=params(),
            name=kernel.__name__,
        )(*arrays)

    kv_blocks = packed(pack_kv, KVR, passage_k, passage_v, new_k, new_v)
    q_blocks = packed(pack_q, HEADS * NT, new_q)

    flat = ctx * 16 + head
    padded = jnp.concatenate([jnp.full((512,), -1, jnp.int32), segments])
    around = lax.dynamic_slice_in_dim(padded, flat // 4 * 256, 768, 0)
    seg_q = lax.dynamic_slice_in_dim(segments, flat * PT, PT, 0)
    start = jnp.sum((around[None, :] < seg_q[:, None]).astype(jnp.int32), axis=1, keepdims=True)

    own = jnp.concatenate([passage_k, passage_v], axis=1)
    kv0, q_blocks, own, start = together(exchange(kv_blocks), q_blocks, own, start)
    kv0_other = permute(kv0, SIBLING)
    left = permute(kv0, along_x(1))
    right = permute(kv0, along_x(3))
    q, left, right = together(exchange(q_blocks), left, right)
    back1, back2 = permute(own, BACK1), permute(own, BACK2)

    far = [permute(left[:16], along_x(1)), permute(right[16:], along_x(3))]
    near = [(kv0, kv0_other, 0, 0)]
    near += [(b, permute(b, SIBLING), 0, d) for b, d in ((left, 3), (right, 1))]
    state = ask(q, near, None, False)
    *far, back1, back2, state = together(*far, back1, back2, state)
    across = permute(jnp.concatenate([back1, jnp.where(y_hi == 0, own, back2)]), OTHER_Y)
    column = jnp.concatenate([own, back1, back2])
    column_other = permute(column, SIBLING)
    far = [(b, permute(b, SIBLING), 16 * i, 2) for i, b in enumerate(far)]
    out_rows = ask(q, far, state, True)
    across, column_other, out_rows = together(across, column_other, out_rows)
    wins = [column, across, column_other, permute(across, SIBLING)]
    new_blocks = exchange(out_rows.reshape(PEERS, HEADS * NT, HD))
    pass_out = passages(passage_q, start, wins)
    pass_out, new_blocks = together(pass_out, new_blocks)
    new_out = new_blocks.reshape(2, KVH, 2, HEADS, NT, HD).transpose(4, 1, 0, 2, 3, 5)
    new_out = new_out.reshape(NT, QH * HD)
    return pass_out, new_out


def solution(mesh):
    row = P(BOTH, None)
    return jax.shard_map(
        on_device,
        mesh=mesh,
        in_specs=(row,) * 6 + (P(),),
        out_specs=(row, row),
        check_vma=False,
    )
```

```python
import functools

import jax
import jax.numpy as jnp
from jax import lax
from jax.experimental import pallas as pl
from jax.experimental.pallas import tpu as pltpu
from jax.sharding import PartitionSpec as P

QH, KVH, HD = 128, 8, 128
GROUP = QH // KVH
PT, NT = 64, 16
BOTH = ("ctx", "head")
COUNT = 128
PEERS = 32
HEADS = 4
ROWS = PEERS * HEADS * NT
KVR = 80
BF, F32 = jnp.bfloat16, jnp.float32
NEG = -1e30
SCALE = HD**-0.5 * 1.4426950408889634
VM = pl.BlockSpec(memory_space=pltpu.VMEM)

GROUPS = [[(y * 4 + x) * 16 + h for y in range(2) for h in range(16)] for x in range(4)]
SIBLING = [(i, i ^ 1) for i in range(COUNT)]
OTHER_Y = [(i, i ^ 2) for i in range(COUNT)]
BACK1 = [(i, i + 4) for i in range(COUNT - 4)]
BACK2 = [(i, i + 8) for i in range(COUNT - 8)]


def along_x(d):
    return [(i, (i // 64) * 64 + (i // 16 + d) % 4 * 16 + i % 16) for i in range(COUNT)]


def params(**kw):
    return pltpu.CompilerParams(vmem_limit_bytes=56 * 2**20, **kw)


def pack_kv(k_ref, v_ref, nk_ref, nv_ref, out_ref):
    for j in range(KVH):
        cols = slice(j * HD, (j + 1) * HD)
        for core in range(2):
            half = slice(32 * core, 32 * core + 32)
            new = nv_ref if core else nk_ref
            for y in range(2):
                d = y * 16 + j * 2 + core
                out_ref[d, 0:32, :] = k_ref[half, cols]
                out_ref[d, 32:64, :] = v_ref[half, cols]
                out_ref[d, 64:80, :] = new[:, cols]


def head_of(d, h):
    y, j, core = d // 16, d % 16 // 2, d % 2
    return j * GROUP + (y * 2 + core) * HEADS + h


def pack_q(q_ref, out_ref):
    for d in range(PEERS):
        for h in range(HEADS):
            g = head_of(d, h)
            out_ref[d, h * NT : (h + 1) * NT, :] = q_ref[:, g * HD : (g + 1) * HD]


RB, KT = 512, 512
BLOCKS = ROWS // RB
STATE = 2 * HD


def pipelined(stages, blocks, tiles, state, unroll=1):
    def step(t, option, fill=True, first=False):
        for r in range(blocks):
            for lag in range(stages):
                at = r - lag
                if at >= 0:
                    if fill:
                        state(lag, t, at, option)
                elif not first:
                    state(lag, t - 1, at + blocks, option)

    for n, (start, end, option) in enumerate(tiles):
        if n == 0:
            step(start, option, first=True)
            start += 1
        if end - start == 1:
            step(start, option)
        elif end > start:
            lax.fori_loop(start, end, lambda t, c, o=option: (step(t, o), c)[1], 0, unroll=unroll)
    step(tiles[-1][1], tiles[-1][2], fill=False)


def question(pieces, first, last, *refs):
    q_ref, refs = refs[0], refs[1:]
    kv, refs = refs[: 2 * len(pieces)], refs[2 * len(pieces) :]
    if not first:
        carry, refs = refs[0], refs[1:]
    out_ref, k_s, v_s, tok_s, s_s, p_s, a_s, m_s = refs[:8]
    total = refs[8] if last else out_ref
    core, x = lax.axis_index("head") % 2, lax.axis_index("ctx") % 4

    def token(src, t, at_x):
        return ((src // 16) * 4 + at_x) * 256 + (src % 16) * 16 + t

    old = sum(2 * peers * 32 for _, peers, _ in pieces)
    at, fresh = 0, old
    tok_s[0] = jnp.full((8, KT), -1, jnp.int32)
    for c, (src0, peers, away) in enumerate(pieces):
        mine, other = kv[2 * c], kv[2 * c + 1]
        for ref in (mine, other):
            rows = slice(at, at + peers * 32)
            k_s[rows, :] = ref[:, 0:32, :].reshape(peers * 32, HD)
            v_s[rows, :HD] = ref[:, 32:64, :].reshape(peers * 32, HD)
            at += peers * 32
        keys = peers * NT
        a = mine[:, 64:80, :].reshape(keys, HD)
        b = other[:, 64:80, :].reshape(keys, HD)
        rows = slice(fresh, fresh + keys)
        k_s[rows, :] = jnp.where(core == 0, a, b)
        v_s[rows, :HD] = jnp.where(core == 0, b, a)
        col = src0 * NT + lax.broadcasted_iota(jnp.int32, (8, keys), 1)
        start = (fresh - old) % KT
        tok_s[1 + (fresh - old) // KT, :, start : start + keys] = token(
            col // 16, col % 16, (x + away) % 4
        )
        fresh += keys
    v_s[:, HD:] = jnp.ones((fresh, HD), BF)
    if first:
        m_s[...] = jnp.full((ROWS, HD), NEG, F32)
        total[...] = jnp.zeros((ROWS, STATE), F32)
    else:
        m_s[...] = jnp.broadcast_to(carry[:, STATE - 1 :], (ROWS, HD))
        total[...] = carry[...]
    old_tiles = old // KT
    lanes = [slice(j * HD, (j + 1) * HD) for j in range(KT // HD)]

    def keys_of(t, width):
        return pl.ds(t * KT if isinstance(t, int) else pl.multiple_of(t * KT, KT), width)

    def stage(which, t, r, masked):
        slot, rows = r % 2, slice(r * RB, (r + 1) * RB)
        early = masked and r < BLOCKS // 2
        width = KT // 2 if early else KT
        half = KT // HD // 2
        if which == 0:
            per = RB // (HEADS * NT)
            q = q_ref[r * per : (r + 1) * per].reshape(RB, HD)
            k = k_s[keys_of(t, width), :]
            s_s[slot, :, :width] = lax.dot_general(
                q, k, (((1,), (1,)), ((), ())), preferred_element_type=F32
            )
        elif which == 1:
            s = [s_s[slot, :, j] for j in lanes[: width // HD]]
            if masked:
                row = r * RB + lax.broadcasted_iota(jnp.int32, (RB, HD), 0)
                q_tok = token(row // 64, row % 16, x)
                for j in range(half) if early else range(half, 2 * half):
                    seen = tok_s[t - old_tiles + 1, 0:1, lanes[j]] <= q_tok
                    s[j] = jnp.where(seen, s[j], NEG)
            top = jnp.max(functools.reduce(jnp.maximum, s), axis=1, keepdims=True)
            before = m_s[rows, :]
            m = jnp.maximum(before, top)
            m_s[rows, :] = m
            a_s[slot] = jnp.exp2((before - m) * SCALE)
            for j, a in zip(lanes, s):
                p_s[slot, :, j] = jnp.exp2((a - m) * SCALE).astype(BF)
        else:
            v = v_s[keys_of(t, width), :]
            pv = jnp.dot(p_s[slot, :, :width], v, preferred_element_type=F32)
            a = a_s[slot]
            total[rows, :HD] = total[rows, :HD] * a + pv[:, :HD]
            total[rows, HD:] = total[rows, HD:] * a + pv[:, HD:]

    pipelined(3, BLOCKS, [(0, old_tiles, False), (old_tiles, fresh // KT, True)], stage, 2)
    if last:
        out_ref[...] = (total[:, :HD] / total[:, HD : HD + 1]).astype(BF)
    else:
        lane = lax.broadcasted_iota(jnp.int32, (ROWS, HD), 1)
        total[:, HD:] = jnp.where(lane == HD - 1, m_s[...], total[:, HD:])


def ask(q, pieces, state, last):
    kinds = tuple((p[2], p[1].shape[0], p[3]) for p in pieces)
    blocks = [b for p in pieces for b in p[:2]]
    keys = sum(80 * k[1] for k in kinds)
    tiles = sum(16 * k[1] for k in kinds) // KT
    scratch = [
        pltpu.VMEM((keys, HD), BF),
        pltpu.VMEM((keys, 2 * HD), BF),
        pltpu.VMEM((1 + tiles, 8, KT), jnp.int32),
        pltpu.VMEM((2, RB, KT), F32),
        pltpu.VMEM((2, RB, KT), BF),
        pltpu.VMEM((2, RB, HD), F32),
        pltpu.VMEM((ROWS, HD), F32),
    ]
    if last:
        scratch.append(pltpu.VMEM((ROWS, STATE), F32))
    carry = [] if state is None else [state]
    return pl.pallas_call(
        functools.partial(question, kinds, state is None, last),
        out_shape=jax.ShapeDtypeStruct((ROWS, HD), BF)
        if last
        else jax.ShapeDtypeStruct((ROWS, STATE), F32),
        in_specs=[VM] * (1 + len(blocks) + len(carry)),
        out_specs=VM,
        scratch_shapes=scratch,
        compiler_params=params(),
        cost_estimate=pl.CostEstimate(
            flops=6 * ROWS * keys * HD, bytes_accessed=4 * 2**20, transcendentals=ROWS * keys
        ),
        name="question",
    )(q, *blocks, *carry)


PARTS, KEYS = 2, 640
PART = GROUP // PARTS


def passage(q_ref, start_ref, *refs):
    wins, o_ref, (bias_ref, s_s, p_s) = refs[:4], refs[4], refs[5:]
    yh, core = lax.axis_index("head") // 2 % 2, lax.axis_index("head") % 2
    col = lax.broadcasted_iota(jnp.int32, (1, KEYS), 1)
    side, blk, t = col // 320, col // 64 % 5, col % 64
    level = jnp.where(blk < 3, 2 - blk, jnp.where(blk == 3, 1, 2 * yh))
    pos = level * 256 + (yh ^ (blk // 3)) * 128 + (core ^ side) * 64 + t
    q_pos = 512 + yh * 128 + core * 64 + lax.broadcasted_iota(jnp.int32, (PT, 1), 0)
    bias_ref[...] = jnp.where((pos <= q_pos) & (pos >= start_ref[...]), 0.0, NEG)
    lanes = [slice(j * HD, (j + 1) * HD) for j in range(KEYS // HD)]

    def columns(j):
        return pl.ds(j * HD if isinstance(j, int) else pl.multiple_of(j * HD, HD), HD)

    def stage(which, j, part, _):
        slot = part % 2
        if which == 0:
            k = jnp.concatenate([w[:, columns(j)] for w in wins], axis=0)
            q = [q_ref[:, columns(j * GROUP + part * PART + h)] for h in range(PART)]
            s_s[slot] = lax.dot_general(
                jnp.concatenate(q, axis=0), k, (((1,), (1,)), ((), ())), preferred_element_type=F32
            )
        elif which == 1:
            for h in range(PART):
                rows = slice(h * PT, (h + 1) * PT)
                s = [s_s[slot, rows, l] + bias_ref[:, l] for l in lanes]
                m = jnp.max(functools.reduce(jnp.maximum, s), axis=1, keepdims=True)
                for l, a in zip(lanes, s):
                    p_s[slot, rows, l] = jnp.exp2((a - m) * SCALE).astype(BF)
        else:
            v = jnp.concatenate([w[:, columns(j + KVH)] for w in wins], axis=0)
            v = jnp.concatenate([v, jnp.ones_like(v)], axis=1)
            o = jnp.dot(p_s[slot], v, preferred_element_type=F32)
            o = (o[:, :HD] / o[:, HD:]).astype(BF)
            for h in range(PART):
                o_ref[:, columns(j * GROUP + part * PART + h)] = o[h * PT : (h + 1) * PT]

    pipelined(3, PARTS, [(0, KVH, None)], stage, 2)


def passages(passage_q, start, wins):
    return pl.pallas_call(
        passage,
        out_shape=jax.ShapeDtypeStruct((PT, QH * HD), BF),
        in_specs=[VM] * 6,
        out_specs=VM,
        scratch_shapes=[
            pltpu.VMEM((PT, KEYS), F32),
            pltpu.VMEM((2, PART * PT, KEYS), F32),
            pltpu.VMEM((2, PART * PT, KEYS), BF),
        ],
        compiler_params=params(),
        cost_estimate=pl.CostEstimate(
            flops=6 * PT * QH * KEYS * HD, bytes_accessed=7 * 2**20, transcendentals=PT * QH * KEYS
        ),
        name="passage",
    )(passage_q, start, *wins)


def permute(block, route):
    return lax.ppermute(block, BOTH, route)


def together(*values):
    return lax.optimization_barrier(values)


def exchange(blocks):
    return lax.all_to_all(
        blocks, BOTH, split_axis=0, concat_axis=0, tiled=True, axis_index_groups=GROUPS
    )


def on_device(passage_q, passage_k, passage_v, new_q, new_k, new_v, segments):
    ctx, head = lax.axis_index("ctx"), lax.axis_index("head")
    y_hi = head // 2 % 2
    shape = jax.ShapeDtypeStruct

    def packed(kernel, rows, *arrays):
        return pl.pallas_call(
            kernel,
            out_shape=shape((PEERS, rows, HD), BF),
            in_specs=[VM] * len(arrays),
            out_specs=VM,
            compiler_params=params(),
            name=kernel.__name__,
        )(*arrays)

    kv_blocks = packed(pack_kv, KVR, passage_k, passage_v, new_k, new_v)
    q_blocks = packed(pack_q, HEADS * NT, new_q)

    flat = ctx * 16 + head
    padded = jnp.concatenate([jnp.full((512,), -1, jnp.int32), segments])
    around = lax.dynamic_slice_in_dim(padded, flat // 4 * 256, 768, 0)
    seg_q = lax.dynamic_slice_in_dim(segments, flat * PT, PT, 0)
    start = jnp.sum((around[None, :] < seg_q[:, None]).astype(jnp.int32), axis=1, keepdims=True)

    own = jnp.concatenate([passage_k, passage_v], axis=1)
    kv0, q_blocks, own, start = together(exchange(kv_blocks), q_blocks, own, start)
    kv0_other = permute(kv0, SIBLING)
    left = permute(kv0, along_x(1))
    right = permute(kv0, along_x(3))
    q, left, right = together(exchange(q_blocks), left, right)
    back1, back2 = permute(own, BACK1), permute(own, BACK2)

    far = [permute(left[:16], along_x(1)), permute(right[16:], along_x(3))]
    near = [(kv0, kv0_other, 0, 0)]
    near += [(b, permute(b, SIBLING), 0, d) for b, d in ((left, 3), (right, 1))]
    state = ask(q, near, None, False)
    *far, back1, back2, state = together(*far, back1, back2, state)
    across = permute(jnp.concatenate([back1, jnp.where(y_hi == 0, own, back2)]), OTHER_Y)
    column = jnp.concatenate([own, back1, back2])
    column_other = permute(column, SIBLING)
    far = [(b, permute(b, SIBLING), 16 * i, 2) for i, b in enumerate(far)]
    out_rows = ask(q, far, state, True)
    across, column_other, out_rows = together(across, column_other, out_rows)
    wins = [column, across, column_other, permute(across, SIBLING)]
    new_blocks = exchange(out_rows.reshape(PEERS, HEADS * NT, HD))
    pass_out = passages(passage_q, start, wins)
    pass_out, new_blocks = together(pass_out, new_blocks)
    new_out = new_blocks.reshape(2, KVH, 2, HEADS, NT, HD).transpose(4, 1, 0, 2, 3, 5)
    new_out = new_out.reshape(NT, QH * HD)
    return pass_out, new_out


def solution(mesh):
    row = P(BOTH, None)
    return jax.shard_map(
        on_device,
        mesh=mesh,
        in_specs=(row,) * 6 + (P(),),
        out_specs=(row, row),
        check_vma=False,
    )
```
